32 devices in a mesh: dp: 8 (over z, y), tensor: 4 (over x, core).
Axes of the slice: x: 2, y: 2, z: 4, core: 2. Of those that a mesh axis runs over, the one named last changes fastest.
Arguments:
- hidden: bfloat16 [128, 4608], P('dp'), may hold values from -6 to 6
- tied_table: bfloat16 [16384, 4608], P(('dp', 'tensor')), may hold values from -0.25 to 0.25
- targets: int32 [128], P('dp'), may hold values from 0 to 16383
- loss_weight: bfloat16 [128], P('dp'), may hold values from 2 to 20
- inputs: int32 [128], P('dp'), may hold values from 0 to 16383
- embed_grad: bfloat16 [128, 4608], P('dp'), may hold values from -0.09375 to 0.09375
Outputs:
- table_grad: bfloat16 [16384, 4608], P(('dp', 'tensor'))
- hidden_grad: float32 [128, 4608], P('dp', 'tensor')
The draws below stay inside these ranges and needn't reach their ends.
All inputs are finite; a program needn't handle non-finite values.
Results may differ from the reference program's by a relative error of at most 0.0052.
Values may be sent and summed in bfloat16 or wider, within the bound.
A program may use at most 64 MiB of HBM per device.

```python
import math
import jax
import jax.numpy as jnp
import numpy as np
from jax import lax

D = 4608
VOCAB = 16384
TOKENS = 128
N_DP = 8


def place_ends(entries, rng, low, largest):
    spot = [jax.random.randint(jax.random.fold_in(rng, axis), (), 0, length) for axis, length in enumerate(entries.shape)]
    longest = entries.shape.index(max(entries.shape))
    neighbour = spot[:longest] + [(spot[longest] + 1) % entries.shape[longest]] + spot[longest + 1:]
    return entries.at[tuple(spot)].set(low).at[tuple(neighbour)].set(largest)


def shard_levels(rng, extent, split, least, largest):
    loudness = 1.0
    for position, parts in split:
        steps = jax.random.uniform(jax.random.fold_in(jax.random.fold_in(rng, 6), position), (parts,), jnp.float32, least / len(split), largest / len(split))
        loudness = loudness * jnp.repeat(jnp.exp(steps), extent[position] // parts).reshape((-1,) + (1,) * (len(extent) - 1 - position))
    return loudness


def cumulative_ranks(amount, lean):
    weights = [(1 << 20) // math.isqrt(rank ** lean) + 1 for rank in range(1, amount + 1)]
    scale = 1 + sum(weights) // (1 << 30)
    return np.cumsum(np.array([max(1, weight // scale) for weight in weights]))


def skewed_ids(stream_key, dims, amount, lean):
    grid = cumulative_ranks(amount, lean)
    pick = jax.random.randint(jax.random.fold_in(stream_key, 1), dims, 0, int(grid[amount - 1]))
    grade = jnp.searchsorted(jnp.asarray(grid, jnp.int32), pick, side="right")
    return jax.random.permutation(jax.random.fold_in(stream_key, 2), amount)[grade].astype(jnp.int32)


def normal_values(stream_key, shape, deviation, reach, split=(), dtype=jnp.bfloat16):
    gain = shard_levels(stream_key, shape, split, -0.22, 0.18) if split else 1.0
    values = jax.random.normal(stream_key, shape, jnp.float32) * deviation * gain
    return jnp.minimum(jnp.maximum(values, -reach), reach).astype(dtype)


def setup_inputs(seed: int = 0) -> dict:
    seeds = jax.random.split(jax.random.key(seed), 7)
    hidden = normal_values(seeds[0], (TOKENS, D), 1.0, 6.0, ((0, 8),))
    tied_table = normal_values(seeds[1], (VOCAB, D), (D // 9) ** -0.5, 0.25, ((0, 32),))
    targets = place_ends(skewed_ids(seeds[2], (TOKENS,), VOCAB, 2), jax.random.fold_in(seeds[2], 3), 0, VOCAB - 1).astype(jnp.int32)
    loss_weight = jnp.clip(jnp.exp(math.log(20.0) - 2.3025851 * jax.random.uniform(seeds[3], (TOKENS,), jnp.float32) ** shard_levels(seeds[3], (TOKENS,), ((0, 8),), -0.2, 0.2)), 2.0, 20.0).astype(jnp.bfloat16)
    inputs = place_ends(skewed_ids(seeds[4], (TOKENS,), VOCAB, 2), jax.random.fold_in(seeds[4], 3), 0, VOCAB - 1).astype(jnp.int32)
    embed_grad = normal_values(seeds[5], (TOKENS, D), D ** -0.5, 0.09375, ((0, 8),))
    return dict(hidden=hidden, tied_table=tied_table, targets=targets, loss_weight=loss_weight, inputs=inputs, embed_grad=embed_grad)


def capped_block(hidden, tied_table, block_index, block_size):
    start = (block_index * block_size).astype(jnp.int32)
    piece = lax.dynamic_slice_in_dim(tied_table, start, block_size, 0)
    logits = lax.dot_general(hidden, piece, (((1,), (1,)), ((), ())), preferred_element_type=jnp.float32)
    return (piece, jnp.tanh(logits / 30.0))

def reference(hidden, tied_table, targets, loss_weight, inputs, embed_grad):
    token_count = hidden.shape[0]
    width = hidden.shape[1]
    vocab_size = tied_table.shape[0]
    block_size = vocab_size // N_DP
    indices = jnp.arange(N_DP).astype(jnp.int32)

    def add_exp(carry, block_index):
        unused, squash = capped_block(hidden, tied_table, block_index, block_size)
        return (carry + lax.optimization_barrier(jnp.sum(jnp.exp(30.0 * squash), axis=1)), None)
    total, unused = lax.scan(add_exp, jnp.zeros((token_count,), jnp.float32), indices)
    weights = loss_weight.astype(jnp.float32)

    def backward(carry, block_index):
        piece, squash = capped_block(hidden, tied_table, block_index, block_size)
        columns = (block_index * block_size + jnp.arange(block_size)).astype(jnp.int32)
        hits = (targets[:, None] == columns[None, :]).astype(jnp.float32)
        probs = jnp.exp(30.0 * squash) / total[:, None]
        dlogit = (weights[:, None] * (probs - hits) * (1.0 - squash * squash)).astype(jnp.bfloat16)
        carry = carry + jnp.dot(dlogit, piece, preferred_element_type=jnp.float32)
        head_term = lax.dot_general(dlogit, hidden, (((0,), (0,)), ((), ())), preferred_element_type=jnp.float32)
        onehot = (inputs[None, :] == columns[:, None]).astype(jnp.bfloat16)
        embed_term = jnp.dot(onehot, embed_grad, preferred_element_type=jnp.float32)
        return (carry, (head_term + math.sqrt(width) * embed_term).astype(jnp.bfloat16))
    hidden_grad, stacked = lax.scan(backward, jnp.zeros((token_count, width), jnp.float32), indices)
    return (stacked.reshape(vocab_size, width), hidden_grad)
```

```python
import functools
import math

import jax
import jax.numpy as jnp
from jax import lax
from jax.experimental import pallas as pl
from jax.experimental.pallas import tpu as pltpu
from jax.sharding import PartitionSpec as P

MESH = pl.DeviceIdType.MESH
ROWS = (((0,), (0,)), ((), ()))
LANES = (((1,), (1,)), ((), ()))


def kernel(
    n_dp, n_t, scale,
    hid, emb, meta, table, tg, hg,
    ha, ea, ma, tab, tgb, sq, dl, oh, dlt, sa, sd, pf, pb, r1, qb, r2, gb, r3,
    h_z, h_y, h_s, h_r, h_r2, e_z, e_y, e_s, e_r, e_r2, m_z, m_y, m_r,
    sa_s, sa_r, sd_s, sd_r, a_s, a_r, b_s, b_r, c_s, c_r, tab_s, tg_s,
):
    d, t = lax.axis_index("dp"), lax.axis_index("tensor")
    n_a, n_x = n_dp // 2, n_t // 2
    a, b = lax.div(d, 2), lax.rem(d, 2)
    x, c = lax.div(t, 2), lax.rem(t, 2)
    side, sib = a * 2 + 1 - b, x * 2 + 1 - c
    rows, width = hid.shape
    half = width // 2
    tokens = n_dp * rows
    vocab = tab.shape[0]
    cols = width // n_t

    load = pltpu.make_async_copy(table, tab, tab_s)
    load.start()
    for h in range(2):
        ha[h, d] = hid[:, h * half:(h + 1) * half]
        ea[h, d] = emb[:, h * half:(h + 1) * half]
    ma[d] = meta[...]

    barrier = pltpu.get_barrier_semaphore()
    for j in range(1, n_t):
        pl.semaphore_signal(barrier, inc=1, device_id=(d, lax.rem(t + j, n_t)), device_id_type=MESH)
    for j in range(1, n_dp):
        pl.semaphore_signal(barrier, inc=1, device_id=(lax.rem(d + j, n_dp), t), device_id_type=MESH)
    pl.semaphore_wait(barrier, n_t + n_dp - 2)

    sent = []

    def send(ref, dst, ss, rs, dev):
        copy = pltpu.make_async_remote_copy(
            src_ref=ref, dst_ref=dst, send_sem=ss, recv_sem=rs, device_id=dev, device_id_type=MESH
        )
        copy.start()
        sent.append(copy)

    def arrived(ref, ss, rs):
        pltpu.make_async_remote_copy(
            src_ref=ref, dst_ref=ref, send_sem=ss, recv_sem=rs, device_id=(side, t), device_id_type=MESH
        ).wait_recv()

    def up(j):
        return lax.rem(a + j, n_a) * 2 + b

    def down(j):
        return lax.rem(a + n_a - j, n_a) * 2

    def gather_start(buf, z, y, r):
        for j in range(1, n_a):
            send(buf.at[c, d], buf.at[c, d], z.at[j], r.at[d], (up(j), t))
        send(buf.at[c, d], buf.at[c, d], y.at[0], r.at[d], (side, t))

    def gather_far(buf, z, y, s, r, r2):
        for j in range(1, n_a):
            k = down(j) + b
            arrived(buf.at[c, k], z.at[j], r.at[k])
            send(buf.at[c, k], buf.at[c, k], y.at[j], r.at[k], (side, t))
            send(buf.at[c, k], buf.at[c, k], s.at[k], r2.at[k], (d, sib))

    def gather_side(buf, z, s, r, r2):
        for j in range(n_a):
            k = down(j) + 1 - b
            arrived(buf.at[c, k], z.at[0], r.at[k])
            send(buf.at[c, k], buf.at[c, k], s.at[k], r2.at[k], (d, sib))

    def gather_end(buf, z, r2):
        for j in range(1, n_dp):
            k = lax.rem(d + j, n_dp)
            arrived(buf.at[1 - c, k], z.at[0], r2.at[k])

    for j in range(1, n_a):
        send(ma.at[d], ma.at[d], m_z.at[j], m_r.at[d], (up(j), t))
    send(ma.at[d], ma.at[d], m_y.at[0], m_r.at[d], (side, t))
    gather_start(ha, h_z, h_y, h_r)
    gather_far(ha, h_z, h_y, h_s, h_r, h_r2)
    for j in range(1, n_a):
        k = down(j) + b
        arrived(ma.at[k], m_z.at[0], m_r.at[k])
        send(ma.at[k], ma.at[k], m_y.at[j], m_r.at[k], (side, t))
    gather_side(ha, h_z, h_s, h_r, h_r2)
    gather_start(ea, e_z, e_y, e_r)
    gather_end(ha, h_z, h_r2)
    load.wait()

    piece = min(vocab, 256)
    left = ha[0].reshape(tokens, half)
    right = ha[1].reshape(tokens, half)

    def logit_rows(i, acc):
        at = pl.ds(pl.multiple_of(i * piece, piece), piece)
        logits = lax.dot_general(tab[at, :half], left, LANES, preferred_element_type=jnp.float32)
        logits += lax.dot_general(tab[at, half:], right, LANES, preferred_element_type=jnp.float32)
        squash = jnp.tanh(logits / 30.0)
        sq[at, :] = squash
        return acc + jnp.sum(jnp.exp(30.0 * squash), axis=0, keepdims=True)

    part = lax.fori_loop(0, vocab // piece, logit_rows, jnp.zeros((1, tokens), jnp.float32))
    sa[t] = jnp.broadcast_to(part, (8, tokens))
    for j in range(1, n_t):
        send(sa.at[t], sa.at[t], sa_s.at[j], sa_r.at[t], (d, lax.rem(t + j, n_t)))
    for j in range(1, n_a):
        k = down(j) + 1 - b
        arrived(ma.at[k], m_z.at[0], m_r.at[k])
    arrived(ma.at[side], m_z.at[0], m_r.at[side])
    for j in range(1, n_t):
        k = lax.rem(t + j, n_t)
        arrived(sa.at[k], sa_s.at[0], sa_r.at[k])
    sd[d] = jnp.sum(sa[...], axis=0)
    for j in range(1, n_dp):
        send(sd.at[d], sd.at[d], sd_s.at[j], sd_r.at[d], (lax.rem(d + j, n_dp), t))
    gather_far(ea, e_z, e_y, e_s, e_r, e_r2)
    ids = jnp.transpose(ma[...].reshape(tokens, 128))
    base = (d * n_t + t) * vocab
    column = (base + lax.broadcasted_iota(jnp.int32, (vocab, tokens), 0)).astype(jnp.float32)
    oh[...] = jnp.where(column == ids[1:2, :], 1.0, 0.0).astype(jnp.bfloat16)
    for j in range(1, n_dp):
        k = lax.rem(d + j, n_dp)
        arrived(sd.at[k], sd_s.at[0], sd_r.at[k])
    total = jnp.sum(sd[...], axis=0)[0:1, :]
    squash = sq[...]
    hits = jnp.where(column == ids[0:1, :], 1.0, 0.0)
    dlogit = ids[2:3, :] * (jnp.exp(30.0 * squash) / total - hits) * (1.0 - squash * squash)
    dl[...] = dlogit.astype(jnp.bfloat16)
    dlt[...] = jnp.transpose(dlogit).astype(jnp.bfloat16)

    for u in range(n_x):
        for v in range(2):
            k = 2 * u + v
            term = jnp.dot(
                dlt[...], tab[:, k * cols:(k + 1) * cols], preferred_element_type=jnp.float32
            )
            pf[k] = term
            pb[k] = term.astype(jnp.bfloat16)
        send(pb.at[2 * u + 1 - c], r1.at[u], a_s.at[u], a_r.at[u], (d, sib))
    for j in list(range(1, n_x)) + [0]:
        u = lax.rem(x + j, n_x)
        arrived(r1.at[u], a_s.at[0], a_r.at[u])
        pair = pf[2 * u + c] + r1[u].astype(jnp.float32)
        if j:
            qb[u] = pair.astype(jnp.bfloat16)
            send(qb.at[u], r2.at[x], b_s.at[j], b_r.at[x], (d, u * 2 + c))
        else:
            pf[2 * u + c] = pair
    gather_side(ea, e_z, e_s, e_r, e_r2)
    gather_end(ea, e_z, e_r2)

    step = 256
    stores = []

    def table_half(h):
        def table_cols(i, carry):
            at = pl.ds(pl.multiple_of(i * step, step), step)
            head = jnp.dot(
                dl[...], ha[h, :, :, at].reshape(tokens, step), preferred_element_type=jnp.float32
            )
            tail = jnp.dot(
                oh[...], ea[h, :, :, at].reshape(tokens, step), preferred_element_type=jnp.float32
            )
            tgb[h, :, at] = (head + scale * tail).astype(jnp.bfloat16)
            return carry

        lax.fori_loop(0, half // step, table_cols, 0)
        copy = pltpu.make_async_copy(tgb.at[h], tg.at[:, h * half:(h + 1) * half], tg_s.at[h])
        copy.start()
        stores.append(copy)

    table_half(0)
    mine = pf[2 * x + c]
    for j in range(1, n_x):
        u = lax.rem(x + j, n_x)
        arrived(r2.at[u], b_s.at[0], b_r.at[u])
        mine = mine + r2[u].astype(jnp.float32)
    pf[2 * x + c] = mine
    gb[...] = mine.reshape(n_dp, rows, cols).astype(jnp.bfloat16)
    for j in range(1, n_dp):
        k = lax.rem(d + j, n_dp)
        send(gb.at[k], r3.at[d], c_s.at[j], c_r.at[d], (k, t))
    table_half(1)
    out = pf[2 * x + c, pl.ds(pl.multiple_of(d * rows, rows), rows), :]
    for j in range(1, n_dp):
        k = lax.rem(d + j, n_dp)
        arrived(r3.at[k], c_s.at[0], c_r.at[k])
        out = out + r3[k].astype(jnp.float32)
    hg[...] = out
    for copy in sent:
        copy.wait_send()
    for copy in stores:
        copy.wait()


def per_device(n_dp, n_t, hidden, tied_table, targets, loss_weight, inputs, embed_grad):
    rows, width = hidden.shape
    vocab = tied_table.shape[0]
    tokens, half, cols, n_x = n_dp * rows, width // 2, width // n_t, n_t // 2
    f32, bf16 = jnp.float32, jnp.bfloat16
    lane = lax.broadcasted_iota(jnp.int32, (rows, 128), 1)
    meta = jnp.where(
        lane == 0,
        targets.astype(f32)[:, None],
        jnp.where(lane == 1, inputs.astype(f32)[:, None], loss_weight.astype(f32)[:, None]),
    )
    vmem = pl.BlockSpec(memory_space=pltpu.VMEM)
    dma = lambda n: pltpu.SemaphoreType.DMA((n,))
    n_a = n_dp // 2
    gather_sems = [dma(n_a), dma(n_a), dma(n_dp), dma(n_dp), dma(n_dp)]
    return pl.pallas_call(
        functools.partial(kernel, n_dp, n_t, math.sqrt(width)),
        out_shape=(
            jax.ShapeDtypeStruct((vocab, width), bf16),
            jax.ShapeDtypeStruct((rows, cols), f32),
        ),
        in_specs=[vmem, vmem, vmem, pl.BlockSpec(memory_space=pl.ANY)],
        out_specs=(pl.BlockSpec(memory_space=pl.ANY), vmem),
        scratch_shapes=[
            pltpu.VMEM((2, n_dp, rows, half), bf16),
            pltpu.VMEM((2, n_dp, rows, half), bf16),
            pltpu.VMEM((n_dp, rows, 128), f32),
            pltpu.VMEM((vocab, width), bf16),
            pltpu.VMEM((2, vocab, half), bf16),
            pltpu.VMEM((vocab, tokens), f32),
            pltpu.VMEM((vocab, tokens), bf16),
            pltpu.VMEM((vocab, tokens), bf16),
            pltpu.VMEM((tokens, vocab), bf16),
            pltpu.VMEM((n_t, 8, tokens), f32),
            pltpu.VMEM((n_dp, 8, tokens), f32),
            pltpu.VMEM((n_t, tokens, cols), f32),
            pltpu.VMEM((n_t, tokens, cols), bf16),
            pltpu.VMEM((n_x, tokens, cols), bf16),
            pltpu.VMEM((n_x, tokens, cols), bf16),
            pltpu.VMEM((n_x, tokens, cols), bf16),
            pltpu.VMEM((n_dp, rows, cols), bf16),
            pltpu.VMEM((n_dp, rows, cols), bf16),
            *gather_sems, *gather_sems,
            dma(n_a), dma(n_a), dma(n_dp),
            dma(n_t), dma(n_t), dma(n_dp), dma(n_dp),
            dma(n_x), dma(n_x), dma(n_x), dma(n_x), dma(n_dp), dma(n_dp),
            pltpu.SemaphoreType.DMA, dma(2),
        ],
        compiler_params=pltpu.CompilerParams(
            collective_id=0, has_side_effects=True, vmem_limit_bytes=56 << 20
        ),
    )(hidden, embed_grad, meta, tied_table)


def solution(mesh):
    placed = (P("dp", None), P(("dp", "tensor"), None), P("dp"), P("dp"), P("dp"), P("dp", None))
    return jax.shard_map(
        functools.partial(per_device, mesh.shape["dp"], mesh.shape["tensor"]),
        mesh=mesh,
        in_specs=placed,
        out_specs=(P(("dp", "tensor"), None), P("dp", "tensor")),
        check_vma=False,
    )
```

```python
import functools
import math

import jax
import jax.numpy as jnp
from jax import lax
from jax.experimental import pallas as pl
from jax.experimental.pallas import tpu as pltpu
from jax.sharding import PartitionSpec as P

MESH = pl.DeviceIdType.MESH
ROWS = (((0,), (0,)), ((), ()))
LANES = (((1,), (1,)), ((), ()))


def kernel(
    n_dp, n_t, scale,
    hid, emb, targets, inputs, weights, table, tg, hg,
    ha, ea, ma, ids, tab, sq, dl, oh, dlt, sa, sd, terms, pf, pb, r1, qb, r2, gb, r3,
    h_z, h_y, h_s, h_r, h_r2, e_z, e_y, e_s, e_r, e_r2, m_z, m_y, m_r,
    sa_s, sa_r, sd_s, sd_r, a_s, a_r, b_s, b_r, c_s, c_r, tab_s,
):
    d, t = lax.axis_index("dp"), lax.axis_index("tensor")
    n_a, n_x = n_dp // 2, n_t // 2
    a, b = lax.div(d, 2), lax.rem(d, 2)
    x, c = lax.div(t, 2), lax.rem(t, 2)
    side, sib = a * 2 + 1 - b, x * 2 + 1 - c
    rows, width = hid.shape
    half = width // 2
    tokens = n_dp * rows
    vocab = tab.shape[0]
    cols = width // n_t

    load = pltpu.make_async_copy(table, tab, tab_s)
    load.start()
    for h in range(2):
        ha[h, d] = hid[:, h * half:(h + 1) * half]
        ea[h, d] = emb[:, h * half:(h + 1) * half]
    ma[d] = jnp.zeros(ma.shape[1:], jnp.float32)
    ma[d, 0:1, 0:rows] = targets[...].astype(jnp.float32)
    ma[d, 1:2, 0:rows] = inputs[...].astype(jnp.float32)
    ma[d, 2:3, 0:rows] = weights[...].astype(jnp.float32)

    barrier = pltpu.get_barrier_semaphore()
    for j in range(1, n_t):
        pl.semaphore_signal(barrier, inc=1, device_id=(d, lax.rem(t + j, n_t)), device_id_type=MESH)
    for j in range(1, n_dp):
        pl.semaphore_signal(barrier, inc=1, device_id=(lax.rem(d + j, n_dp), t), device_id_type=MESH)
    pl.semaphore_wait(barrier, n_t + n_dp - 2)

    sent = []

    def send(ref, dst, ss, rs, dev):
        copy = pltpu.make_async_remote_copy(
            src_ref=ref, dst_ref=dst, send_sem=ss, recv_sem=rs, device_id=dev, device_id_type=MESH
        )
        copy.start()
        sent.append(copy)

    def arrived(ref, ss, rs):
        pltpu.make_async_remote_copy(
            src_ref=ref, dst_ref=ref, send_sem=ss, recv_sem=rs, device_id=(side, t), device_id_type=MESH
        ).wait_recv()

    def up(j):
        return lax.rem(a + j, n_a) * 2 + b

    def down(j):
        return lax.rem(a + n_a - j, n_a) * 2

    def gather_start(buf, z, y, r):
        for j in range(1, n_a):
            send(buf.at[c, d], buf.at[c, d], z.at[j], r.at[d], (up(j), t))
        send(buf.at[c, d], buf.at[c, d], y.at[0], r.at[d], (side, t))

    def gather_far(buf, z, y, s, r, r2):
        for j in range(1, n_a):
            k = down(j) + b
            arrived(buf.at[c, k], z.at[j], r.at[k])
            send(buf.at[c, k], buf.at[c, k], y.at[j], r.at[k], (side, t))
            send(buf.at[c, k], buf.at[c, k], s.at[k], r2.at[k], (d, sib))

    def gather_side(buf, z, s, r, r2):
        for j in range(n_a):
            k = down(j) + 1 - b
            arrived(buf.at[c, k], z.at[0], r.at[k])
            send(buf.at[c, k], buf.at[c, k], s.at[k], r2.at[k], (d, sib))

    def gather_end(buf, z, r2):
        for j in range(1, n_dp):
            k = lax.rem(d + j, n_dp)
            arrived(buf.at[1 - c, k], z.at[0], r2.at[k])

    for j in range(1, n_a):
        send(ma.at[d], ma.at[d], m_z.at[j], m_r.at[d], (up(j), t))
    send(ma.at[d], ma.at[d], m_y.at[0], m_r.at[d], (side, t))
    gather_start(ha, h_z, h_y, h_r)
    gather_far(ha, h_z, h_y, h_s, h_r, h_r2)
    for j in range(1, n_a):
        k = down(j) + b
        arrived(ma.at[k], m_z.at[0], m_r.at[k])
        send(ma.at[k], ma.at[k], m_y.at[j], m_r.at[k], (side, t))
    gather_side(ha, h_z, h_s, h_r, h_r2)
    gather_start(ea, e_z, e_y, e_r)
    load.wait()
    piece = min(vocab, 256)

    def logits(i, core):
        at = pl.ds(pl.multiple_of(i * piece, piece), piece)
        side_cols = pl.ds(pl.multiple_of(core * half, half), half)
        return at, lax.dot_general(
            tab[at, side_cols], ha[core].reshape(tokens, half), LANES,
            preferred_element_type=jnp.float32,
        )

    def first_half(i, carry):
        at, product = logits(i, c)
        sq[at, :] = product
        return carry

    def second_half(i, acc):
        at, product = logits(i, 1 - c)
        squash = jnp.tanh((sq[at, :] + product) / 30.0)
        sq[at, :] = squash
        return acc + jnp.sum(jnp.exp(30.0 * squash), axis=0, keepdims=True)

    lax.fori_loop(0, vocab // piece, first_half, 0)
    gather_end(ha, h_z, h_r2)
    part = lax.fori_loop(0, vocab // piece, second_half, jnp.zeros((1, tokens), jnp.float32))
    sa[t] = jnp.broadcast_to(part, (8, tokens))
    for j in range(1, n_t):
        send(sa.at[t], sa.at[t], sa_s.at[j], sa_r.at[t], (d, lax.rem(t + j, n_t)))
    for j in range(1, n_a):
        k = down(j) + 1 - b
        arrived(ma.at[k], m_z.at[0], m_r.at[k])
    arrived(ma.at[side], m_z.at[0], m_r.at[side])
    for j in range(1, n_t):
        k = lax.rem(t + j, n_t)
        arrived(sa.at[k], sa_s.at[0], sa_r.at[k])
    sd[d] = jnp.sum(sa[...], axis=0)
    for j in range(1, n_dp):
        send(sd.at[d], sd.at[d], sd_s.at[j], sd_r.at[d], (lax.rem(d + j, n_dp), t))
    gather_far(ea, e_z, e_y, e_s, e_r, e_r2)
    for k in range(n_dp):
        ids[:, k * rows:(k + 1) * rows] = ma[k, :, 0:rows]
    base = (d * n_t + t) * vocab
    column = (base + lax.broadcasted_iota(jnp.int32, (vocab, tokens), 0)).astype(jnp.float32)
    oh[...] = jnp.where(column == ids[1:2, :], 1.0, 0.0).astype(jnp.bfloat16)
    for j in range(1, n_dp):
        k = lax.rem(d + j, n_dp)
        arrived(sd.at[k], sd_s.at[0], sd_r.at[k])
    total = jnp.sum(sd[...], axis=0)[0:1, :]
    squash = sq[...]
    hits = jnp.where(column == ids[0:1, :], 1.0, 0.0)
    dlogit = ids[2:3, :] * (jnp.exp(30.0 * squash) / total - hits) * (1.0 - squash * squash)
    dl[...] = dlogit.astype(jnp.bfloat16)
    dlt[...] = jnp.transpose(dlogit).astype(jnp.bfloat16)

    def term(k):
        return jnp.dot(dlt[...], tab[:, k], preferred_element_type=jnp.float32)

    def columns(k):
        return pl.ds(pl.multiple_of(k * cols, 128), cols)

    aligned = cols % 128 == 0
    if not aligned:
        for k in range(n_t):
            terms[k] = term(slice(k * cols, (k + 1) * cols))
    order = list(range(1, n_x)) + [0]
    for j in order:
        u = lax.rem(x + j, n_x)
        give, keep = 2 * u + 1 - c, 2 * u + c
        pb[u] = (term(columns(give)) if aligned else terms[give]).astype(jnp.bfloat16)
        send(pb.at[u], r1.at[u], a_s.at[u], a_r.at[u], (d, sib))
        pf[u] = term(columns(keep)) if aligned else terms[keep]

    n_q = 2
    slots = n_dp // n_q

    def pair(u, i):
        k = lax.rem(d + 1 + i, n_dp)
        at = pl.ds(pl.multiple_of(k * rows, rows), rows)
        return pf[u, at, :] + r1[u, at, :].astype(jnp.float32)

    for j in order:
        u = lax.rem(x + j, n_x)
        arrived(r1.at[u], a_s.at[0], a_r.at[u])
        if j:
            for q in range(n_q):
                for i in range(q * slots, (q + 1) * slots):
                    qb[u, i] = pair(u, i).astype(jnp.bfloat16)
                span = pl.ds(q * slots, slots)
                send(qb.at[u, span], r2.at[x, span], b_s.at[j, q], b_r.at[x, q], (d, u * 2 + c))
    gather_side(ea, e_z, e_s, e_r, e_r2)
    for q in range(n_q):
        for j in range(1, n_x):
            u = lax.rem(x + j, n_x)
            arrived(r2.at[u, pl.ds(q * slots, slots)], b_s.at[0, 0], b_r.at[u, q])
        for i in range(q * slots, (q + 1) * slots):
            mine = pair(x, i)
            for j in range(1, n_x):
                mine = mine + r2[lax.rem(x + j, n_x), i].astype(jnp.float32)
            if i < n_dp - 1:
                gb[i] = mine.astype(jnp.bfloat16)
                send(gb.at[i], r3.at[d], c_s.at[i], c_r.at[d], (lax.rem(d + 1 + i, n_dp), t))
            else:
                hg[...] = mine
    gather_end(ea, e_z, e_r2)

    step = 256
    for h in range(2):
        def table_cols(i, carry):
            at = pl.ds(pl.multiple_of(i * step, step), step)
            head = jnp.dot(
                dl[...], ha[h, :, :, at].reshape(tokens, step), preferred_element_type=jnp.float32
            )
            tail = jnp.dot(
                oh[...], ea[h, :, :, at].reshape(tokens, step), preferred_element_type=jnp.float32
            )
            place = pl.ds(pl.multiple_of(h * half + i * step, step), step)
            tg[:, place] = (head + scale * tail).astype(jnp.bfloat16)
            return carry

        lax.fori_loop(0, half // step, table_cols, 0)

    out = hg[...]
    for j in range(1, n_dp):
        k = lax.rem(d + j, n_dp)
        arrived(r3.at[k], c_s.at[0], c_r.at[k])
        out = out + r3[k].astype(jnp.float32)
    hg[...] = out
    for copy in sent:
        copy.wait_send()


def per_device(n_dp, n_t, hidden, tied_table, targets, loss_weight, inputs, embed_grad):
    rows, width = hidden.shape
    vocab = tied_table.shape[0]
    tokens, half, cols, n_x = n_dp * rows, width // 2, width // n_t, n_t // 2
    f32, bf16 = jnp.float32, jnp.bfloat16
    vmem = pl.BlockSpec(memory_space=pltpu.VMEM)
    dma = lambda n: pltpu.SemaphoreType.DMA((n,))
    n_a = n_dp // 2
    gather_sems = [dma(n_a), dma(n_a), dma(n_dp), dma(n_dp), dma(n_dp)]
    return pl.pallas_call(
        functools.partial(kernel, n_dp, n_t, math.sqrt(width)),
        out_shape=(
            pltpu.VMEM((vocab, width), bf16),
            pltpu.VMEM((rows, cols), f32),
        ),
        in_specs=[vmem] * 5 + [pl.BlockSpec(memory_space=pl.ANY)],
        out_specs=(vmem, vmem),
        scratch_shapes=[
            pltpu.VMEM((2, n_dp, rows, half), bf16),
            pltpu.VMEM((2, n_dp, rows, half), bf16),
            pltpu.VMEM((n_dp, 8, 128), f32),
            pltpu.VMEM((8, tokens), f32),
            pltpu.VMEM((vocab, width), bf16),
            pltpu.VMEM((vocab, tokens), f32),
            pltpu.VMEM((vocab, tokens), bf16),
            pltpu.VMEM((vocab, tokens), bf16),
            pltpu.VMEM((tokens, vocab), bf16),
            pltpu.VMEM((n_t, 8, tokens), f32),
            pltpu.VMEM((n_dp, 8, tokens), f32),
            pltpu.VMEM((n_t, tokens, cols) if cols % 128 else (8, 128), f32),
            pltpu.VMEM((n_x, tokens, cols), f32),
            pltpu.VMEM((n_x, tokens, cols), bf16),
            pltpu.VMEM((n_x, tokens, cols), bf16),
            pltpu.VMEM((n_x, n_dp, rows, cols), bf16),
            pltpu.VMEM((n_x, n_dp, rows, cols), bf16),
            pltpu.VMEM((n_dp, rows, cols), bf16),
            pltpu.VMEM((n_dp, rows, cols), bf16),
            *gather_sems, *gather_sems,
            dma(n_a), dma(n_a), dma(n_dp),
            dma(n_t), dma(n_t), dma(n_dp), dma(n_dp),
            dma(n_x), dma(n_x), pltpu.SemaphoreType.DMA((n_x, 2)), pltpu.SemaphoreType.DMA((n_x, 2)),
            dma(n_dp), dma(n_dp),
            pltpu.SemaphoreType.DMA,
        ],
        compiler_params=pltpu.CompilerParams(
            collective_id=0, has_side_effects=True, vmem_limit_bytes=56 << 20
        ),
    )(hidden, embed_grad, targets[None], inputs[None], loss_weight[None], tied_table)


def solution(mesh):
    placed = (P("dp", None), P(("dp", "tensor"), None), P("dp"), P("dp"), P("dp"), P("dp", None))
    return jax.shard_map(
        functools.partial(per_device, mesh.shape["dp"], mesh.shape["tensor"]),
        mesh=mesh,
        in_specs=placed,
        out_specs=(P(("dp", "tensor"), None), P("dp", "tensor")),
        check_vma=False,
    )
```

```python
import functools
import math

import jax
import jax.numpy as jnp
from jax import lax
from jax.experimental import pallas as pl
from jax.experimental.pallas import tpu as pltpu
from jax.sharding import PartitionSpec as P

MESH = pl.DeviceIdType.MESH
ROWS = (((0,), (0,)), ((), ()))
LANES = (((1,), (1,)), ((), ()))


def kernel(
    n_dp, n_t, scale,
    hid, emb, targets, inputs, weights, table, tg, hg,
    ha, ea, ma, ids, tab, sq, dl, oh, dlt, sa, sd, terms, pf, pb, r1, qb, r2, gb, r3,
    h_z, h_y, h_s, h_r, h_r2, e_z, e_y, e_s, e_r, e_r2, m_z, m_y, m_r,
    sa_s, sa_r, sd_s, sd_r, a_s, a_r, b_s, b_r, c_s, c_r, tab_s,
):
    d, t = lax.axis_index("dp"), lax.axis_index("tensor")
    n_a, n_x = n_dp // 2, n_t // 2
    a, b = lax.div(d, 2), lax.rem(d, 2)
    x, c = lax.div(t, 2), lax.rem(t, 2)
    side, sib = a * 2 + 1 - b, x * 2 + 1 - c
    rows, width = hid.shape
    half = width // 2
    tokens = n_dp * rows
    vocab = tab.shape[0]
    cols = width // n_t

    barrier = pltpu.get_barrier_semaphore()
    for j in range(1, n_t):
        pl.semaphore_signal(barrier, inc=1, device_id=(d, lax.rem(t + j, n_t)), device_id_type=MESH)
    for j in range(1, n_dp):
        pl.semaphore_signal(barrier, inc=1, device_id=(lax.rem(d + j, n_dp), t), device_id_type=MESH)
    load = pltpu.make_async_copy(table, tab, tab_s)
    load.start()
    for h in range(2):
        ha[h, d] = hid[:, h * half:(h + 1) * half]
        ea[h, d] = emb[:, h * half:(h + 1) * half]
    ma[d] = jnp.zeros(ma.shape[1:], jnp.float32)
    ma[d, 0:1, 0:rows] = targets[...].astype(jnp.float32)
    ma[d, 1:2, 0:rows] = inputs[...].astype(jnp.float32)
    ma[d, 2:3, 0:rows] = weights[...].astype(jnp.float32)

    pl.semaphore_wait(barrier, n_t + n_dp - 2)

    sent = []

    def send(ref, dst, ss, rs, dev):
        copy = pltpu.make_async_remote_copy(
            src_ref=ref, dst_ref=dst, send_sem=ss, recv_sem=rs, device_id=dev, device_id_type=MESH
        )
        copy.start()
        sent.append(copy)

    def arrived(ref, ss, rs):
        pltpu.make_async_remote_copy(
            src_ref=ref, dst_ref=ref, send_sem=ss, recv_sem=rs, device_id=(side, t), device_id_type=MESH
        ).wait_recv()

    def up(j):
        return lax.rem(a + j, n_a) * 2 + b

    def down(j):
        return lax.rem(a + n_a - j, n_a) * 2

    def gather_start(buf, z, y, r):
        for j in range(1, n_a):
            send(buf.at[c, d], buf.at[c, d], z.at[j], r.at[d], (up(j), t))
        send(buf.at[c, d], buf.at[c, d], y.at[0], r.at[d], (side, t))

    def gather_far(buf, z, y, s, r, r2):
        for j in range(1, n_a):
            k = down(j) + b
            arrived(buf.at[c, k], z.at[j], r.at[k])
            send(buf.at[c, k], buf.at[c, k], y.at[j], r.at[k], (side, t))
            send(buf.at[c, k], buf.at[c, k], s.at[k], r2.at[k], (d, sib))

    def gather_side(buf, z, s, r, r2):
        for j in range(n_a):
            k = down(j) + 1 - b
            arrived(buf.at[c, k], z.at[0], r.at[k])
            send(buf.at[c, k], buf.at[c, k], s.at[k], r2.at[k], (d, sib))

    def gather_end(buf, z, r2):
        for j in range(1, n_dp):
            k = lax.rem(d + j, n_dp)
            arrived(buf.at[1 - c, k], z.at[0], r2.at[k])

    for j in range(1, n_a):
        send(ma.at[d], ma.at[d], m_z.at[j], m_r.at[d], (up(j), t))
    send(ma.at[d], ma.at[d], m_y.at[0], m_r.at[d], (side, t))
    gather_start(ha, h_z, h_y, h_r)
    gather_far(ha, h_z, h_y, h_s, h_r, h_r2)
    for j in range(1, n_a):
        k = down(j) + b
        arrived(ma.at[k], m_z.at[0], m_r.at[k])
        send(ma.at[k], ma.at[k], m_y.at[j], m_r.at[k], (side, t))
    gather_side(ha, h_z, h_s, h_r, h_r2)
    gather_start(ea, e_z, e_y, e_r)
    load.wait()
    piece = min(vocab, 256)

    def logits(i, core):
        at = pl.ds(pl.multiple_of(i * piece, piece), piece)
        side_cols = pl.ds(pl.multiple_of(core * half, half), half)
        return at, lax.dot_general(
            tab[at, side_cols], ha[core].reshape(tokens, half), LANES,
            preferred_element_type=jnp.float32,
        )

    def first_half(i, carry):
        at, product = logits(i, c)
        sq[at, :] = product
        return carry

    def second_half(i, acc):
        at, product = logits(i, 1 - c)
        squash = jnp.tanh((sq[at, :] + product) / 30.0)
        sq[at, :] = squash
        return acc + jnp.sum(jnp.exp(30.0 * squash), axis=0, keepdims=True)

    lax.fori_loop(0, vocab // piece, first_half, 0)
    gather_end(ha, h_z, h_r2)
    part = lax.fori_loop(0, vocab // piece, second_half, jnp.zeros((1, tokens), jnp.float32))
    sa[t] = jnp.broadcast_to(part, (8, tokens))
    for j in range(1, n_t):
        send(sa.at[t], sa.at[t], sa_s.at[j], sa_r.at[t], (d, lax.rem(t + j, n_t)))
    for j in range(1, n_a):
        k = down(j) + 1 - b
        arrived(ma.at[k], m_z.at[0], m_r.at[k])
    arrived(ma.at[side], m_z.at[0], m_r.at[side])
    for j in range(1, n_t):
        k = lax.rem(t + j, n_t)
        arrived(sa.at[k], sa_s.at[0], sa_r.at[k])
    sd[d] = jnp.sum(sa[...], axis=0)
    for j in range(1, n_dp):
        send(sd.at[d], sd.at[d], sd_s.at[j], sd_r.at[d], (lax.rem(d + j, n_dp), t))
    gather_far(ea, e_z, e_y, e_s, e_r, e_r2)
    for k in range(n_dp):
        ids[:, k * rows:(k + 1) * rows] = ma[k, :, 0:rows]
    base = (d * n_t + t) * vocab
    column = (base + lax.broadcasted_iota(jnp.int32, (vocab, tokens), 0)).astype(jnp.float32)
    oh[...] = jnp.where(column == ids[1:2, :], 1.0, 0.0).astype(jnp.bfloat16)
    for j in range(1, n_dp):
        k = lax.rem(d + j, n_dp)
        arrived(sd.at[k], sd_s.at[0], sd_r.at[k])
    total = jnp.sum(sd[...], axis=0)[0:1, :]
    squash = sq[...]
    hits = jnp.where(column == ids[0:1, :], 1.0, 0.0)
    dlogit = ids[2:3, :] * (jnp.exp(30.0 * squash) / total - hits) * (1.0 - squash * squash)
    dl[...] = dlogit.astype(jnp.bfloat16)
    dlt[...] = jnp.transpose(dlogit).astype(jnp.bfloat16)

    def term(k):
        return jnp.dot(dlt[...], tab[:, k], preferred_element_type=jnp.float32)

    def columns(k):
        return pl.ds(pl.multiple_of(k * cols, 128), cols)

    aligned = cols % 128 == 0
    if not aligned:
        for k in range(n_t):
            terms[k] = term(slice(k * cols, (k + 1) * cols))
    order = list(range(1, n_x)) + [0]
    for j in order:
        u = lax.rem(x + j, n_x)
        give, keep = 2 * u + 1 - c, 2 * u + c
        pb[u] = (term(columns(give)) if aligned else terms[give]).astype(jnp.bfloat16)
        send(pb.at[u], r1.at[u], a_s.at[u], a_r.at[u], (d, sib))
        if j:
            pf[u] = term(columns(keep)) if aligned else terms[keep]

    n_q = 2
    slots = n_dp // n_q

    def pair(u, i):
        k = lax.rem(d + 1 + i, n_dp)
        at = pl.ds(pl.multiple_of(k * rows, rows), rows)
        return pf[u, at, :] + r1[u, at, :].astype(jnp.float32)

    for j in order:
        u = lax.rem(x + j, n_x)
        if j:
            arrived(r1.at[u], a_s.at[0], a_r.at[u])
            for q in range(n_q):
                for i in range(q * slots, (q + 1) * slots):
                    qb[u, i] = pair(u, i).astype(jnp.bfloat16)
                span = pl.ds(q * slots, slots)
                send(qb.at[u, span], r2.at[x, span], b_s.at[j, q], b_r.at[x, q], (d, u * 2 + c))
    arrived(r1.at[x], a_s.at[0], a_r.at[x])
    pf[x] = term(columns(2 * x + c)) if aligned else terms[2 * x + c]
    gather_side(ea, e_z, e_s, e_r, e_r2)
    step = 256

    def table_half(h):
        def table_cols(i, carry):
            at = pl.ds(pl.multiple_of(i * step, step), step)
            head = jnp.dot(
                dl[...], ha[h, :, :, at].reshape(tokens, step), preferred_element_type=jnp.float32
            )
            tail = jnp.dot(
                oh[...], ea[h, :, :, at].reshape(tokens, step), preferred_element_type=jnp.float32
            )
            place = pl.ds(pl.multiple_of(h * half + i * step, step), step)
            tg[:, place] = (head + scale * tail).astype(jnp.bfloat16)
            return carry

        lax.fori_loop(0, half // step, table_cols, 0)

    gather_end(ea, e_z, e_r2)
    table_half(0)
    for q in range(n_q):
        for j in range(1, n_x):
            u = lax.rem(x + j, n_x)
            arrived(r2.at[u, pl.ds(q * slots, slots)], b_s.at[0, 0], b_r.at[u, q])
        for i in range(q * slots, (q + 1) * slots):
            mine = pair(x, i)
            for j in range(1, n_x):
                mine = mine + r2[lax.rem(x + j, n_x), i].astype(jnp.float32)
            if i < n_dp - 1:
                gb[i] = mine.astype(jnp.bfloat16)
                send(gb.at[i], r3.at[d], c_s.at[i], c_r.at[d], (lax.rem(d + 1 + i, n_dp), t))
            else:
                hg[...] = mine

    table_half(1)
    out = hg[...]
    for j in range(1, n_dp):
        k = lax.rem(d + j, n_dp)
        arrived(r3.at[k], c_s.at[0], c_r.at[k])
        out = out + r3[k].astype(jnp.float32)
    hg[...] = out
    for copy in sent:
        copy.wait_send()


def per_device(n_dp, n_t, hidden, tied_table, targets, loss_weight, inputs, embed_grad):
    rows, width = hidden.shape
    vocab = tied_table.shape[0]
    tokens, half, cols, n_x = n_dp * rows, width // 2, width // n_t, n_t // 2
    f32, bf16 = jnp.float32, jnp.bfloat16
    vmem = pl.BlockSpec(memory_space=pltpu.VMEM)
    dma = lambda n: pltpu.SemaphoreType.DMA((n,))
    n_a = n_dp // 2
    gather_sems = [dma(n_a), dma(n_a), dma(n_dp), dma(n_dp), dma(n_dp)]
    return pl.pallas_call(
        functools.partial(kernel, n_dp, n_t, math.sqrt(width)),
        out_shape=(
            pltpu.VMEM((vocab, width), bf16),
            pltpu.VMEM((rows, cols), f32),
        ),
        in_specs=[vmem] * 5 + [pl.BlockSpec(memory_space=pl.ANY)],
        out_specs=(vmem, vmem),
        scratch_shapes=[
            pltpu.VMEM((2, n_dp, rows, half), bf16),
            pltpu.VMEM((2, n_dp, rows, half), bf16),
            pltpu.VMEM((n_dp, 8, 128), f32),
            pltpu.VMEM((8, tokens), f32),
            pltpu.VMEM((vocab, width), bf16),
            pltpu.VMEM((vocab, tokens), f32),
            pltpu.VMEM((vocab, tokens), bf16),
            pltpu.VMEM((vocab, tokens), bf16),
            pltpu.VMEM((tokens, vocab), bf16),
            pltpu.VMEM((n_t, 8, tokens), f32),
            pltpu.VMEM((n_dp, 8, tokens), f32),
            pltpu.VMEM((n_t, tokens, cols) if cols % 128 else (8, 128), f32),
            pltpu.VMEM((n_x, tokens, cols), f32),
            pltpu.VMEM((n_x, tokens, cols), bf16),
            pltpu.VMEM((n_x, tokens, cols), bf16),
            pltpu.VMEM((n_x, n_dp, rows, cols), bf16),
            pltpu.VMEM((n_x, n_dp, rows, cols), bf16),
            pltpu.VMEM((n_dp, rows, cols), bf16),
            pltpu.VMEM((n_dp, rows, cols), bf16),
            *gather_sems, *gather_sems,
            dma(n_a), dma(n_a), dma(n_dp),
            dma(n_t), dma(n_t), dma(n_dp), dma(n_dp),
            dma(n_x), dma(n_x), pltpu.SemaphoreType.DMA((n_x, 2)), pltpu.SemaphoreType.DMA((n_x, 2)),
            dma(n_dp), dma(n_dp),
            pltpu.SemaphoreType.DMA,
        ],
        compiler_params=pltpu.CompilerParams(
            collective_id=0, has_side_effects=True, vmem_limit_bytes=56 << 20
        ),
    )(hidden, embed_grad, targets[None], inputs[None], loss_weight[None], tied_table)


def solution(mesh):
    placed = (P("dp", None), P(("dp", "tensor"), None), P("dp"), P("dp"), P("dp"), P("dp", None))
    return jax.shard_map(
        functools.partial(per_device, mesh.shape["dp"], mesh.shape["tensor"]),
        mesh=mesh,
        in_specs=placed,
        out_specs=(P(("dp", "tensor"), None), P("dp", "tensor")),
        check_vma=False,
    )
```

```python
import functools
import math

import jax
import jax.numpy as jnp
from jax import lax
from jax.experimental import pallas as pl
from jax.experimental.pallas import tpu as pltpu
from jax.sharding import PartitionSpec as P

MESH = pl.DeviceIdType.MESH
ROWS = (((0,), (0,)), ((), ()))
LANES = (((1,), (1,)), ((), ()))


def kernel(
    n_dp, n_t, scale,
    hid, emb, targets, inputs, weights, table, tg, hg,
    ha, ea, ma, ids, tab, sq, dl, oh, dlt, sa, sd, terms, pf, pb, r1, qb, r2, gb, r3,
    h_z, h_y, h_s, h_r, h_r2, e_z, e_y, e_s, e_r, e_r2, m_z, m_y, m_r,
    sa_s, sa_r, sd_s, sd_r, a_s, a_r, b_s, b_r, c_s, c_r, tab_s,
):
    d, t = lax.axis_index("dp"), lax.axis_index("tensor")
    n_a, n_x = n_dp // 2, n_t // 2
    a, b = lax.div(d, 2), lax.rem(d, 2)
    x, c = lax.div(t, 2), lax.rem(t, 2)
    side, sib = a * 2 + 1 - b, x * 2 + 1 - c
    rows, width = hid.shape
    half = width // 2
    tokens = n_dp * rows
    vocab = tab.shape[0]
    cols = width // n_t

    barrier = pltpu.get_barrier_semaphore()
    for j in range(1, n_t):
        pl.semaphore_signal(barrier, inc=1, device_id=(d, lax.rem(t + j, n_t)), device_id_type=MESH)
    for j in range(1, n_dp):
        pl.semaphore_signal(barrier, inc=1, device_id=(lax.rem(d + j, n_dp), t), device_id_type=MESH)
    load = pltpu.make_async_copy(table, tab, tab_s)
    load.start()
    for h in range(2):
        ha[h, d] = hid[:, h * half:(h + 1) * half]
        ea[h, d] = emb[:, h * half:(h + 1) * half]
    ma[d] = jnp.zeros(ma.shape[1:], jnp.float32)
    ma[d, 0:1, 0:rows] = targets[...].astype(jnp.float32)
    ma[d, 1:2, 0:rows] = inputs[...].astype(jnp.float32)
    ma[d, 2:3, 0:rows] = weights[...].astype(jnp.float32)

    pl.semaphore_wait(barrier, n_t + n_dp - 2)

    sent = []

    def send(ref, dst, ss, rs, dev):
        copy = pltpu.make_async_remote_copy(
            src_ref=ref, dst_ref=dst, send_sem=ss, recv_sem=rs, device_id=dev, device_id_type=MESH
        )
        copy.start()
        sent.append(copy)

    def arrived(ref, ss, rs):
        pltpu.make_async_remote_copy(
            src_ref=ref, dst_ref=ref, send_sem=ss, recv_sem=rs, device_id=(side, t), device_id_type=MESH
        ).wait_recv()

    def up(j):
        return lax.rem(a + j, n_a) * 2 + b

    def down(j):
        return lax.rem(a + n_a - j, n_a) * 2

    def gather_start(buf, z, y, r):
        for j in range(1, n_a):
            send(buf.at[c, d], buf.at[c, d], z.at[j], r.at[d], (up(j), t))
        send(buf.at[c, d], buf.at[c, d], y.at[0], r.at[d], (side, t))

    def gather_far(buf, z, y, s, r, r2):
        for j in range(1, n_a):
            k = down(j) + b
            arrived(buf.at[c, k], z.at[j], r.at[k])
            send(buf.at[c, k], buf.at[c, k], y.at[j], r.at[k], (side, t))
            send(buf.at[c, k], buf.at[c, k], s.at[k], r2.at[k], (d, sib))

    def gather_side(buf, z, s, r, r2):
        for j in range(n_a):
            k = down(j) + 1 - b
            arrived(buf.at[c, k], z.at[0], r.at[k])
            send(buf.at[c, k], buf.at[c, k], s.at[k], r2.at[k], (d, sib))

    def gather_end(buf, z, r2):
        for j in range(1, n_dp):
            k = lax.rem(d + j, n_dp)
            arrived(buf.at[1 - c, k], z.at[0], r2.at[k])

    e = lax.rem(x, 2)
    across = (x + 1 - 2 * e) * 2 + c
    quarter = half // 2

    def cut(k, part):
        return ha.at[c, k, :, pl.ds(pl.multiple_of(part * quarter, 128), quarter)]

    for j in range(1, n_a):
        send(cut(d, e), cut(d, e), h_z.at[j], h_r.at[d], (up(j), t))
    send(ha.at[c, d], ha.at[c, d], h_y.at[0], h_r.at[d], (side, t))
    for j in range(1, n_a):
        k = down(j) + b
        arrived(cut(k, e), h_z.at[0], h_r.at[k])
        send(cut(k, e), cut(k, e), h_z.at[n_a + j], h_r.at[n_dp + k], (d, across))
        send(cut(k, e), cut(k, e), h_y.at[j], h_r.at[k], (side, t))
    for j in range(1, n_a):
        k = down(j) + b
        arrived(cut(k, 1 - e), h_z.at[0], h_r.at[n_dp + k])
        send(cut(k, 1 - e), cut(k, 1 - e), h_y.at[n_a + j], h_r.at[n_dp + k], (side, t))
        send(ha.at[c, k], ha.at[c, k], h_s.at[k], h_r2.at[k], (d, sib))
    for j in range(n_a):
        k = down(j) + 1 - b
        if j:
            arrived(cut(k, e), h_z.at[0], h_r.at[k])
            arrived(cut(k, 1 - e), h_z.at[0], h_r.at[n_dp + k])
        else:
            arrived(ha.at[c, k], h_z.at[0], h_r.at[k])
        send(ha.at[c, k], ha.at[c, k], h_s.at[k], h_r2.at[k], (d, sib))
    for j in range(1, n_a):
        send(ma.at[d], ma.at[d], m_z.at[j], m_r.at[d], (up(j), t))
    send(ma.at[d], ma.at[d], m_y.at[0], m_r.at[d], (side, t))
    gather_start(ea, e_z, e_y, e_r)
    load.wait()
    piece = min(vocab, 256)

    def logits(i, core):
        at = pl.ds(pl.multiple_of(i * piece, piece), piece)
        side_cols = pl.ds(pl.multiple_of(core * half, half), half)
        return at, lax.dot_general(
            tab[at, side_cols], ha[core].reshape(tokens, half), LANES,
            preferred_element_type=jnp.float32,
        )

    def first_half(i, carry):
        at, product = logits(i, c)
        sq[at, :] = product
        return carry

    def second_half(i, acc):
        at, product = logits(i, 1 - c)
        squash = jnp.tanh((sq[at, :] + product) / 30.0)
        sq[at, :] = squash
        return acc + jnp.sum(jnp.exp(30.0 * squash), axis=0, keepdims=True)

    lax.fori_loop(0, vocab // piece, first_half, 0)
    gather_end(ha, h_z, h_r2)
    part = lax.fori_loop(0, vocab // piece, second_half, jnp.zeros((1, tokens), jnp.float32))
    sa[t] = jnp.broadcast_to(part, (8, tokens))
    for j in range(1, n_t):
        send(sa.at[t], sa.at[t], sa_s.at[j], sa_r.at[t], (d, lax.rem(t + j, n_t)))
    for j in range(1, n_a):
        k = down(j) + b
        arrived(ma.at[k], m_z.at[0], m_r.at[k])
        send(ma.at[k], ma.at[k], m_y.at[j], m_r.at[k], (side, t))
    for j in range(1, n_t):
        k = lax.rem(t + j, n_t)
        arrived(sa.at[k], sa_s.at[0], sa_r.at[k])
    sd[d] = jnp.sum(sa[...], axis=0)
    for j in range(1, n_dp):
        send(sd.at[d], sd.at[d], sd_s.at[j], sd_r.at[d], (lax.rem(d + j, n_dp), t))
    gather_far(ea, e_z, e_y, e_s, e_r, e_r2)
    for j in range(1, n_a):
        k = down(j) + 1 - b
        arrived(ma.at[k], m_z.at[0], m_r.at[k])
    arrived(ma.at[side], m_z.at[0], m_r.at[side])
    for k in range(n_dp):
        ids[:, k * rows:(k + 1) * rows] = ma[k, :, 0:rows]
    base = (d * n_t + t) * vocab
    column = (base + lax.broadcasted_iota(jnp.int32, (vocab, tokens), 0)).astype(jnp.float32)
    oh[...] = jnp.where(column == ids[1:2, :], 1.0, 0.0).astype(jnp.bfloat16)
    for j in range(1, n_dp):
        k = lax.rem(d + j, n_dp)
        arrived(sd.at[k], sd_s.at[0], sd_r.at[k])
    total = jnp.sum(sd[...], axis=0)[0:1, :]
    squash = sq[...]
    hits = jnp.where(column == ids[0:1, :], 1.0, 0.0)
    dlogit = ids[2:3, :] * (jnp.exp(30.0 * squash) / total - hits) * (1.0 - squash * squash)
    dl[...] = dlogit.astype(jnp.bfloat16)
    dlt[...] = jnp.transpose(dlogit).astype(jnp.bfloat16)

    def term(k):
        return jnp.dot(dlt[...], tab[:, k], preferred_element_type=jnp.float32)

    def columns(k):
        return pl.ds(pl.multiple_of(k * cols, 128), cols)

    aligned = cols % 128 == 0
    if not aligned:
        for k in range(n_t):
            terms[k] = term(slice(k * cols, (k + 1) * cols))
    order = list(range(1, n_x)) + [0]
    for j in order:
        u = lax.rem(x + j, n_x)
        give, keep = 2 * u + 1 - c, 2 * u + c
        pb[u] = (term(columns(give)) if aligned else terms[give]).astype(jnp.bfloat16)
        send(pb.at[u], r1.at[u], a_s.at[u], a_r.at[u], (d, sib))
        if j:
            pf[u] = term(columns(keep)) if aligned else terms[keep]

    n_q = 2
    slots = n_dp // n_q

    def pair(u, i):
        k = lax.rem(d + 1 + i, n_dp)
        at = pl.ds(pl.multiple_of(k * rows, rows), rows)
        return pf[u, at, :] + r1[u, at, :].astype(jnp.float32)

    for j in order:
        u = lax.rem(x + j, n_x)
        if j:
            arrived(r1.at[u], a_s.at[0], a_r.at[u])
            for q in range(n_q):
                for i in range(q * slots, (q + 1) * slots):
                    qb[u, i] = pair(u, i).astype(jnp.bfloat16)
                span = pl.ds(q * slots, slots)
                send(qb.at[u, span], r2.at[x, span], b_s.at[j, q], b_r.at[x, q], (d, u * 2 + c))
    arrived(r1.at[x], a_s.at[0], a_r.at[x])
    pf[x] = term(columns(2 * x + c)) if aligned else terms[2 * x + c]
    gather_side(ea, e_z, e_s, e_r, e_r2)
    step = 256

    def table_half(h):
        def table_cols(i, carry):
            at = pl.ds(pl.multiple_of(i * step, step), step)
            head = jnp.dot(
                dl[...], ha[h, :, :, at].reshape(tokens, step), preferred_element_type=jnp.float32
            )
            tail = jnp.dot(
                oh[...], ea[h, :, :, at].reshape(tokens, step), preferred_element_type=jnp.float32
            )
            place = pl.ds(pl.multiple_of(h * half + i * step, step), step)
            tg[:, place] = (head + scale * tail).astype(jnp.bfloat16)
            return carry

        lax.fori_loop(0, half // step, table_cols, 0)

    gather_end(ea, e_z, e_r2)
    table_half(0)
    for q in range(n_q):
        for j in range(1, n_x):
            u = lax.rem(x + j, n_x)
            arrived(r2.at[u, pl.ds(q * slots, slots)], b_s.at[0, 0], b_r.at[u, q])
        for i in range(q * slots, (q + 1) * slots):
            mine = pair(x, i)
            for j in range(1, n_x):
                mine = mine + r2[lax.rem(x + j, n_x), i].astype(jnp.float32)
            if i < n_dp - 1:
                gb[i] = mine.astype(jnp.bfloat16)
                send(gb.at[i], r3.at[d], c_s.at[i], c_r.at[d], (lax.rem(d + 1 + i, n_dp), t))
            else:
                hg[...] = mine

    table_half(1)
    out = hg[...]
    for j in range(1, n_dp):
        k = lax.rem(d + j, n_dp)
        arrived(r3.at[k], c_s.at[0], c_r.at[k])
        out = out + r3[k].astype(jnp.float32)
    hg[...] = out
    for copy in sent:
        copy.wait_send()


def per_device(n_dp, n_t, hidden, tied_table, targets, loss_weight, inputs, embed_grad):
    rows, width = hidden.shape
    vocab = tied_table.shape[0]
    tokens, half, cols, n_x = n_dp * rows, width // 2, width // n_t, n_t // 2
    f32, bf16 = jnp.float32, jnp.bfloat16
    vmem = pl.BlockSpec(memory_space=pltpu.VMEM)
    dma = lambda n: pltpu.SemaphoreType.DMA((n,))
    n_a = n_dp // 2
    gather_sems = [dma(n_a), dma(n_a), dma(n_dp), dma(n_dp), dma(n_dp)]
    return pl.pallas_call(
        functools.partial(kernel, n_dp, n_t, math.sqrt(width)),
        out_shape=(
            pltpu.VMEM((vocab, width), bf16),
            pltpu.VMEM((rows, cols), f32),
        ),
        in_specs=[vmem] * 5 + [pl.BlockSpec(memory_space=pl.ANY)],
        out_specs=(vmem, vmem),
        scratch_shapes=[
            pltpu.VMEM((2, n_dp, rows, half), bf16),
            pltpu.VMEM((2, n_dp, rows, half), bf16),
            pltpu.VMEM((n_dp, 8, 128), f32),
            pltpu.VMEM((8, tokens), f32),
            pltpu.VMEM((vocab, width), bf16),
            pltpu.VMEM((vocab, tokens), f32),
            pltpu.VMEM((vocab, tokens), bf16),
            pltpu.VMEM((vocab, tokens), bf16),
            pltpu.VMEM((tokens, vocab), bf16),
            pltpu.VMEM((n_t, 8, tokens), f32),
            pltpu.VMEM((n_dp, 8, tokens), f32),
            pltpu.VMEM((n_t, tokens, cols) if cols % 128 else (8, 128), f32),
            pltpu.VMEM((n_x, tokens, cols), f32),
            pltpu.VMEM((n_x, tokens, cols), bf16),
            pltpu.VMEM((n_x, tokens, cols), bf16),
            pltpu.VMEM((n_x, n_dp, rows, cols), bf16),
            pltpu.VMEM((n_x, n_dp, rows, cols), bf16),
            pltpu.VMEM((n_dp, rows, cols), bf16),
            pltpu.VMEM((n_dp, rows, cols), bf16),
            dma(2 * n_a), dma(2 * n_a), dma(n_dp), dma(2 * n_dp), dma(n_dp), *gather_sems,
            dma(n_a), dma(n_a), dma(n_dp),
            dma(n_t), dma(n_t), dma(n_dp), dma(n_dp),
            dma(n_x), dma(n_x), pltpu.SemaphoreType.DMA((n_x, 2)), pltpu.SemaphoreType.DMA((n_x, 2)),
            dma(n_dp), dma(n_dp),
            pltpu.SemaphoreType.DMA,
        ],
        compiler_params=pltpu.CompilerParams(
            collective_id=0, has_side_effects=True, vmem_limit_bytes=56 << 20
        ),
    )(hidden, embed_grad, targets[None], inputs[None], loss_weight[None], tied_table)


def solution(mesh):
    placed = (P("dp", None), P(("dp", "tensor"), None), P("dp"), P("dp"), P("dp"), P("dp", None))
    return jax.shard_map(
        functools.partial(per_device, mesh.shape["dp"], mesh.shape["tensor"]),
        mesh=mesh,
        in_specs=placed,
        out_specs=(P(("dp", "tensor"), None), P("dp", "tensor")),
        check_vma=False,
    )
```

```python
import functools
import math

import jax
import jax.numpy as jnp
from jax import lax
from jax.experimental import pallas as pl
from jax.experimental.pallas import tpu as pltpu
from jax.sharding import PartitionSpec as P

MESH = pl.DeviceIdType.MESH
ROWS = (((0,), (0,)), ((), ()))
LANES = (((1,), (1,)), ((), ()))


def kernel(
    n_dp, n_t, scale,
    hid, emb, targets, inputs, weights, table, tg, hg,
    ha, ea, ma, ids, tab, sq, dl, oh, dlt, sa, sd, terms, pf, pb, r1, qb, r2, gb, r3,
    h_z, h_y, h_s, h_r, h_r2, e_z, e_y, e_s, e_r, e_r2, m_z, m_y, m_r,
    sa_s, sa_r, sd_s, sd_r, a_s, a_r, b_s, b_r, c_s, c_r, tab_s,
):
    d, t = lax.axis_index("dp"), lax.axis_index("tensor")
    n_a, n_x = n_dp // 2, n_t // 2
    a, b = lax.div(d, 2), lax.rem(d, 2)
    x, c = lax.div(t, 2), lax.rem(t, 2)
    side, sib = a * 2 + 1 - b, x * 2 + 1 - c
    rows, width = hid.shape
    half = width // 2
    tokens = n_dp * rows
    vocab = tab.shape[0]
    cols = width // n_t

    barrier = pltpu.get_barrier_semaphore()
    for j in range(1, n_t):
        pl.semaphore_signal(barrier, inc=1, device_id=(d, lax.rem(t + j, n_t)), device_id_type=MESH)
    for j in range(1, n_dp):
        pl.semaphore_signal(barrier, inc=1, device_id=(lax.rem(d + j, n_dp), t), device_id_type=MESH)
    load = pltpu.make_async_copy(table, tab, tab_s)
    load.start()
    for h in range(2):
        ha[h, d] = hid[:, h * half:(h + 1) * half]
        ea[h, d] = emb[:, h * half:(h + 1) * half]
    ma[d] = jnp.zeros(ma.shape[1:], jnp.float32)
    ma[d, 0:1, 0:rows] = targets[...].astype(jnp.float32)
    ma[d, 1:2, 0:rows] = inputs[...].astype(jnp.float32)
    ma[d, 2:3, 0:rows] = weights[...].astype(jnp.float32)

    pl.semaphore_wait(barrier, n_t + n_dp - 2)

    sent = []

    def send(ref, dst, ss, rs, dev):
        copy = pltpu.make_async_remote_copy(
            src_ref=ref, dst_ref=dst, send_sem=ss, recv_sem=rs, device_id=dev, device_id_type=MESH
        )
        copy.start()
        sent.append(copy)

    def arrived(ref, ss, rs):
        pltpu.make_async_remote_copy(
            src_ref=ref, dst_ref=ref, send_sem=ss, recv_sem=rs, device_id=(side, t), device_id_type=MESH
        ).wait_recv()

    def up(j):
        return lax.rem(a + j, n_a) * 2 + b

    def down(j):
        return lax.rem(a + n_a - j, n_a) * 2

    def gather_start(buf, z, y, r):
        for j in range(1, n_a):
            send(buf.at[c, d], buf.at[c, d], z.at[j], r.at[d], (up(j), t))
        send(buf.at[c, d], buf.at[c, d], y.at[0], r.at[d], (side, t))

    def gather_far(buf, z, y, s, r, r2):
        for j in range(1, n_a):
            k = down(j) + b
            arrived(buf.at[c, k], z.at[j], r.at[k])
            send(buf.at[c, k], buf.at[c, k], y.at[j], r.at[k], (side, t))
            send(buf.at[c, k], buf.at[c, k], s.at[k], r2.at[k], (d, sib))

    def gather_side(buf, z, s, r, r2):
        for j in range(n_a):
            k = down(j) + 1 - b
            arrived(buf.at[c, k], z.at[0], r.at[k])
            send(buf.at[c, k], buf.at[c, k], s.at[k], r2.at[k], (d, sib))

    def gather_end(buf, z, r2):
        for j in range(1, n_dp):
            k = lax.rem(d + j, n_dp)
            arrived(buf.at[1 - c, k], z.at[0], r2.at[k])

    e = lax.rem(x, 2)
    across = (x + 1 - 2 * e) * 2 + c
    quarter = half // 2

    def cut(k, part):
        return ha.at[c, k, :, pl.ds(pl.multiple_of(part * quarter, 128), quarter)]

    for j in range(1, n_a):
        send(cut(d, e), cut(d, e), h_z.at[j], h_r.at[d], (up(j), t))
    send(ha.at[c, d], ha.at[c, d], h_y.at[0], h_r.at[d], (side, t))
    for j in range(1, n_a):
        k = down(j) + b
        arrived(cut(k, e), h_z.at[0], h_r.at[k])
        send(cut(k, e), cut(k, e), h_z.at[n_a + j], h_r.at[n_dp + k], (d, across))
        send(cut(k, e), cut(k, e), h_y.at[j], h_r.at[k], (side, t))
    for j in range(1, n_a):
        k = down(j) + b
        arrived(cut(k, 1 - e), h_z.at[0], h_r.at[n_dp + k])
        send(cut(k, 1 - e), cut(k, 1 - e), h_y.at[n_a + j], h_r.at[n_dp + k], (side, t))
        send(ha.at[c, k], ha.at[c, k], h_s.at[k], h_r2.at[k], (d, sib))
    for j in range(n_a):
        k = down(j) + 1 - b
        if j:
            arrived(cut(k, e), h_z.at[0], h_r.at[k])
            arrived(cut(k, 1 - e), h_z.at[0], h_r.at[n_dp + k])
        else:
            arrived(ha.at[c, k], h_z.at[0], h_r.at[k])
        send(ha.at[c, k], ha.at[c, k], h_s.at[k], h_r2.at[k], (d, sib))
    for j in range(1, n_a):
        send(ma.at[d], ma.at[d], m_z.at[j], m_r.at[d], (up(j), t))
    send(ma.at[d], ma.at[d], m_y.at[0], m_r.at[d], (side, t))
    gather_start(ea, e_z, e_y, e_r)
    load.wait()
    piece = min(vocab, 256)

    def logits(i, core):
        at = pl.ds(pl.multiple_of(i * piece, piece), piece)
        side_cols = pl.ds(pl.multiple_of(core * half, half), half)
        return at, lax.dot_general(
            tab[at, side_cols], ha[core].reshape(tokens, half), LANES,
            preferred_element_type=jnp.float32,
        )

    def first_half(i, carry):
        at, product = logits(i, c)
        sq[at, :] = product
        return carry

    def second_half(i, acc):
        at, product = logits(i, 1 - c)
        squash = jnp.tanh((sq[at, :] + product) / 30.0)
        sq[at, :] = squash
        return acc + jnp.sum(jnp.exp(30.0 * squash), axis=0, keepdims=True)

    lax.fori_loop(0, vocab // piece, first_half, 0)
    gather_end(ha, h_z, h_r2)
    part = lax.fori_loop(0, vocab // piece, second_half, jnp.zeros((1, tokens), jnp.float32))
    sa[t] = jnp.broadcast_to(part, (8, tokens))
    for j in range(1, n_t):
        send(sa.at[t], sa.at[t], sa_s.at[j], sa_r.at[t], (d, lax.rem(t + j, n_t)))
    for j in range(1, n_a):
        k = down(j) + b
        arrived(ma.at[k], m_z.at[0], m_r.at[k])
        send(ma.at[k], ma.at[k], m_y.at[j], m_r.at[k], (side, t))
    for j in range(1, n_t):
        k = lax.rem(t + j, n_t)
        arrived(sa.at[k], sa_s.at[0], sa_r.at[k])
    sd[d] = jnp.sum(sa[...], axis=0)
    for j in range(1, n_dp):
        send(sd.at[d], sd.at[d], sd_s.at[j], sd_r.at[d], (lax.rem(d + j, n_dp), t))
    gather_far(ea, e_z, e_y, e_s, e_r, e_r2)
    for j in range(1, n_a):
        k = down(j) + 1 - b
        arrived(ma.at[k], m_z.at[0], m_r.at[k])
    arrived(ma.at[side], m_z.at[0], m_r.at[side])
    for k in range(n_dp):
        ids[:, k * rows:(k + 1) * rows] = ma[k, :, 0:rows]
    base = (d * n_t + t) * vocab
    column = (base + lax.broadcasted_iota(jnp.int32, (vocab, tokens), 0)).astype(jnp.float32)
    oh[...] = jnp.where(column == ids[1:2, :], 1.0, 0.0).astype(jnp.bfloat16)
    for j in range(1, n_dp):
        k = lax.rem(d + j, n_dp)
        arrived(sd.at[k], sd_s.at[0], sd_r.at[k])
    total = jnp.sum(sd[...], axis=0)[0:1, :]
    squash = sq[...]
    hits = jnp.where(column == ids[0:1, :], 1.0, 0.0)
    dlogit = ids[2:3, :] * (jnp.exp(30.0 * squash) / total - hits) * (1.0 - squash * squash)
    dl[...] = dlogit.astype(jnp.bfloat16)
    dlt[...] = jnp.transpose(dlogit).astype(jnp.bfloat16)

    def term(k):
        return jnp.dot(dlt[...], tab[:, k], preferred_element_type=jnp.float32)

    def columns(k):
        return pl.ds(pl.multiple_of(k * cols, 128), cols)

    aligned = cols % 128 == 0
    if not aligned:
        for k in range(n_t):
            terms[k] = term(slice(k * cols, (k + 1) * cols))
    order = list(range(1, n_x)) + [0]
    for j in order:
        u = lax.rem(x + j, n_x)
        give, keep = 2 * u + 1 - c, 2 * u + c
        pb[u] = (term(columns(give)) if aligned else terms[give]).astype(jnp.bfloat16)
        send(pb.at[u], r1.at[u], a_s.at[u], a_r.at[u], (d, sib))
        if j:
            pf[u] = term(columns(keep)) if aligned else terms[keep]

    n_q = 4
    slots = n_dp // n_q

    def pair(u, i):
        k = lax.rem(d + 1 + i, n_dp)
        at = pl.ds(pl.multiple_of(k * rows, rows), rows)
        return pf[u, at, :] + r1[u, at, :].astype(jnp.float32)

    for j in order:
        u = lax.rem(x + j, n_x)
        if j:
            arrived(r1.at[u], a_s.at[0], a_r.at[u])
            for q in range(n_q):
                for i in range(q * slots, (q + 1) * slots):
                    qb[u, i] = pair(u, i).astype(jnp.bfloat16)
                span = pl.ds(q * slots, slots)
                send(qb.at[u, span], r2.at[x, span], b_s.at[j, q], b_r.at[x, q], (d, u * 2 + c))
    arrived(r1.at[x], a_s.at[0], a_r.at[x])
    pf[x] = term(columns(2 * x + c)) if aligned else terms[2 * x + c]
    gather_side(ea, e_z, e_s, e_r, e_r2)
    step = 256

    def table_half(h):
        def table_cols(i, carry):
            at = pl.ds(pl.multiple_of(i * step, step), step)
            head = jnp.dot(
                dl[...], ha[h, :, :, at].reshape(tokens, step), preferred_element_type=jnp.float32
            )
            tail = jnp.dot(
                oh[...], ea[h, :, :, at].reshape(tokens, step), preferred_element_type=jnp.float32
            )
            place = pl.ds(pl.multiple_of(h * half + i * step, step), step)
            tg[:, place] = (head + scale * tail).astype(jnp.bfloat16)
            return carry

        lax.fori_loop(0, half // step, table_cols, 0)

    gather_end(ea, e_z, e_r2)
    table_half(0)
    for q in range(n_q):
        for j in range(1, n_x):
            u = lax.rem(x + j, n_x)
            arrived(r2.at[u, pl.ds(q * slots, slots)], b_s.at[0, 0], b_r.at[u, q])
        for i in range(q * slots, (q + 1) * slots):
            mine = pair(x, i)
            for j in range(1, n_x):
                mine = mine + r2[lax.rem(x + j, n_x), i].astype(jnp.float32)
            if i < n_dp - 1:
                gb[i] = mine.astype(jnp.bfloat16)
                send(gb.at[i], r3.at[d], c_s.at[i], c_r.at[d], (lax.rem(d + 1 + i, n_dp), t))
            else:
                hg[...] = mine

    table_half(1)
    out = hg[...]
    for j in range(1, n_dp):
        k = lax.rem(d + j, n_dp)
        arrived(r3.at[k], c_s.at[0], c_r.at[k])
        out = out + r3[k].astype(jnp.float32)
    hg[...] = out
    for copy in sent:
        copy.wait_send()


def per_device(n_dp, n_t, hidden, tied_table, targets, loss_weight, inputs, embed_grad):
    rows, width = hidden.shape
    vocab = tied_table.shape[0]
    tokens, half, cols, n_x = n_dp * rows, width // 2, width // n_t, n_t // 2
    f32, bf16 = jnp.float32, jnp.bfloat16
    vmem = pl.BlockSpec(memory_space=pltpu.VMEM)
    dma = lambda n: pltpu.SemaphoreType.DMA((n,))
    n_a = n_dp // 2
    gather_sems = [dma(n_a), dma(n_a), dma(n_dp), dma(n_dp), dma(n_dp)]
    return pl.pallas_call(
        functools.partial(kernel, n_dp, n_t, math.sqrt(width)),
        out_shape=(
            pltpu.VMEM((vocab, width), bf16),
            pltpu.VMEM((rows, cols), f32),
        ),
        in_specs=[vmem] * 5 + [pl.BlockSpec(memory_space=pl.ANY)],
        out_specs=(vmem, vmem),
        scratch_shapes=[
            pltpu.VMEM((2, n_dp, rows, half), bf16),
            pltpu.VMEM((2, n_dp, rows, half), bf16),
            pltpu.VMEM((n_dp, 8, 128), f32),
            pltpu.VMEM((8, tokens), f32),
            pltpu.VMEM((vocab, width), bf16),
            pltpu.VMEM((vocab, tokens), f32),
            pltpu.VMEM((vocab, tokens), bf16),
            pltpu.VMEM((vocab, tokens), bf16),
            pltpu.VMEM((tokens, vocab), bf16),
            pltpu.VMEM((n_t, 8, tokens), f32),
            pltpu.VMEM((n_dp, 8, tokens), f32),
            pltpu.VMEM((n_t, tokens, cols) if cols % 128 else (8, 128), f32),
            pltpu.VMEM((n_x, tokens, cols), f32),
            pltpu.VMEM((n_x, tokens, cols), bf16),
            pltpu.VMEM((n_x, tokens, cols), bf16),
            pltpu.VMEM((n_x, n_dp, rows, cols), bf16),
            pltpu.VMEM((n_x, n_dp, rows, cols), bf16),
            pltpu.VMEM((n_dp, rows, cols), bf16),
            pltpu.VMEM((n_dp, rows, cols), bf16),
            dma(2 * n_a), dma(2 * n_a), dma(n_dp), dma(2 * n_dp), dma(n_dp), *gather_sems,
            dma(n_a), dma(n_a), dma(n_dp),
            dma(n_t), dma(n_t), dma(n_dp), dma(n_dp),
            dma(n_x), dma(n_x), pltpu.SemaphoreType.DMA((n_x, 4)), pltpu.SemaphoreType.DMA((n_x, 4)),
            dma(n_dp), dma(n_dp),
            pltpu.SemaphoreType.DMA,
        ],
        compiler_params=pltpu.CompilerParams(
            collective_id=0, has_side_effects=True, vmem_limit_bytes=56 << 20
        ),
    )(hidden, embed_grad, targets[None], inputs[None], loss_weight[None], tied_table)


def solution(mesh):
    placed = (P("dp", None), P(("dp", "tensor"), None), P("dp"), P("dp"), P("dp"), P("dp", None))
    return jax.shard_map(
        functools.partial(per_device, mesh.shape["dp"], mesh.shape["tensor"]),
        mesh=mesh,
        in_specs=placed,
        out_specs=(P(("dp", "tensor"), None), P("dp", "tensor")),
        check_vma=False,
    )
```
